512 devices in a mesh: seg: 32 (over y, x, core), head: 16 (over z).
Axes of the slice: x: 4, y: 4, z: 16, core: 2. Of those that a mesh axis runs over, the one named last changes fastest.
Arguments:
- queries: bfloat16 [16384, 4096], P('seg', 'head'), may hold values from -6 to 6
- key_tokens: bfloat16 [16384, 4096], P('seg', 'head'), may hold values from -0.52734375 to 0.52734375
- values: bfloat16 [16384, 4096], P('seg', 'head'), may hold values from -6 to 6
- upstream: bfloat16 [16384, 4096], P('seg', 'head'), may hold values from -6 to 6
- norm_gain: float32 [4096], P('head'), may hold values from 0.1 to 1.9
- decay_rate: float32 [32], P('head'), may hold values from 3.0517579e-06 to 0.00390625
- block_length: int32 [32], replicated, may hold values from 1 to 512, 12288 in all
- parent: int32 [32], replicated, may hold values from -1 to 30, as said below
Outputs:
- attention_out: bfloat16 [16384, 4096], P('seg', 'head')
- query_grad: bfloat16 [16384, 4096], P('seg', 'head')
- key_grad: bfloat16 [16384, 4096], P('seg', 'head')
- value_grad: bfloat16 [16384, 4096], P('seg', 'head')
The draws below stay inside these ranges and needn't reach their ends.
Inputs may be any that keep to these rules, and one draw needn't show every extreme that they name: parent[0] is -1; every other block's parent is -1 or an earlier block, and block 31 always continues block 30.
All inputs are finite; a program needn't handle non-finite values.
Results may differ from the reference program's by a relative error of at most 0.012.
Values sent between devices are 32-bit elements; how exact they have to be, the bound alone decides.
A program may use at most 64 MiB of HBM per device.

```python
import math
import jax
import jax.numpy as jnp
import numpy as np
from jax import lax

HEADS = 32
DH = 128
TOK_DEV = 512
BLOCKS = 32
TOKENS = 16384


def draw_parent(key, part):
    indices = jnp.arange(BLOCKS, dtype=jnp.int32)
    kinds = jax.random.randint(jax.random.fold_in(key, 11), (BLOCKS,), 0, 8)
    distant = jax.random.randint(jax.random.fold_in(key, 12), (BLOCKS,), 0, jnp.maximum(indices, 1))
    parent = jnp.where(kinds == 0, -1, jnp.where(kinds < 5, indices - 1, distant))
    parent = jnp.where(indices == 0, -1, parent)
    parent = jnp.where(indices == BLOCKS - 1, BLOCKS - 2, parent)
    return parent.astype(jnp.int32)


def levels(rng, extent, split, smallest, high):
    def one(axis_at, blocks):
        draws = jax.random.uniform(jax.random.fold_in(jax.random.fold_in(rng, 6), axis_at), (blocks,), jnp.float32, smallest / len(split), high / len(split))
        return jnp.repeat(jnp.exp(draws), extent[axis_at] // blocks).reshape((-1,) + (1,) * (len(extent) - axis_at - 1))

    gain = one(*split[0])
    for cut in split[1:]:
        gain = gain * one(*cut)
    return gain


def split_up(number_of, total, bound, lean):
    weights = [(1 << 20) // math.isqrt(rank ** lean) + 1 for rank in range(2, number_of + 1)]
    spare, holding = total - bound - (number_of - 1), [1] * (number_of - 1)
    while spare > 0:
        movable = [i for i in range(number_of - 1) if holding[i] < bound]
        whole, left = sum([weights[i] for i in movable]), spare
        for i in movable:
            addition = min(bound - holding[i], max(1, left * weights[i] // whole), spare)
            holding[i] = holding[i] + addition
            spare = spare - addition
    return np.array([bound] + holding)


def ragged(rng, number_of, total, reach, slope):
    if number_of == 2:
        one = jax.random.randint(rng, (), max(1, total - reach), min(reach, total - 1) + 1)
        return jnp.stack([one, total - one])
    tallies = jnp.asarray(split_up(number_of, total, reach, slope), jnp.int32)
    couples = (number_of - 1) // 2
    giver, sink = tallies[1:1 + 2 * couples:2], tallies[2:2 + 2 * couples:2]
    margin = jnp.minimum(giver - 1, reach - sink)
    moved = jax.random.randint(jax.random.fold_in(rng, 1), (couples,), 0, 1 << 20) % (margin + 1)
    tallies = tallies.at[1:1 + 2 * couples:2].set(giver - moved).at[2:2 + 2 * couples:2].set(sink + moved)
    return tallies[jax.random.permutation(jax.random.fold_in(rng, 2), number_of)]


def scatter_about(rng, dims, spread, reach, cuts=(), kind=jnp.bfloat16):
    values = jax.random.normal(rng, dims, jnp.float32) * spread
    if len(cuts) > 0:
        values = levels(rng, dims, cuts, -0.22, 0.18) * values
    return jnp.clip(values, min=-reach, max=reach).astype(kind)


def setup_inputs(seed: int = 0) -> dict:
    key_list = jax.random.split(jax.random.key(seed), 9)
    return {
        "queries": scatter_about(key_list[0], (TOKENS, HEADS * DH), 1.0, 6.0, ((0, 32), (1, 16))),
        "key_tokens": scatter_about(key_list[1], (TOKENS, HEADS * DH), (DH ** -0.5), 0.52734375, ((0, 32), (1, 16))),
        "values": scatter_about(key_list[2], (TOKENS, HEADS * DH), 1.0, 6.0, ((0, 32), (1, 16))),
        "upstream": scatter_about(key_list[3], (TOKENS, HEADS * DH), 1.0, 6.0, ((0, 32), (1, 16))),
        "norm_gain": jnp.clip(1.0 + 0.18 * jax.random.normal(key_list[4], (HEADS * DH,), jnp.float32), 0.1, 1.9),
        "decay_rate": jnp.clip(jnp.exp(math.log(0.00390625) - 7.1546153 * jax.random.uniform(key_list[5], (HEADS,), jnp.float32) ** levels(key_list[5], (HEADS,), ((0, 16),), -0.2, 0.2)), 3.051757857974735e-06, 0.00390625),
        "block_length": ragged(key_list[6], BLOCKS, BLOCKS * TOK_DEV * 3 // 4, TOK_DEV, 1).astype(jnp.int32),
        "parent": draw_parent(jax.random.fold_in(key_list[8], 71), 0),
    }


norm_eps = 1e-05
highest = lax.Precision.HIGHEST

def ancestry(block_length, parent, decay_rate):
    count = parent.shape[0]
    columns = jnp.arange(count, dtype=jnp.int32)
    linked = (parent[:, None] == columns[None, :]).astype(jnp.float32)
    for step in range(max(1, (count - 1).bit_length())):
        linked = jnp.minimum(linked + jnp.dot(linked, linked, precision=highest), 1.0)
    lengths = block_length.astype(jnp.float32)
    depth = jnp.dot(linked, lengths, precision=highest)
    distance = jnp.maximum(depth[:, None] - depth[None, :] - lengths[None, :], 0.0)
    decayed = jnp.exp(-distance[:, :, None] * decay_rate[None, None, :])
    return jnp.where(linked[:, :, None] > 0.5, decayed, 0.0)

def block_local(query_full, key_full, value_full, length, decay_rate):
    row_count, width_here = query_full.shape
    heads_here = decay_rate.shape[0]
    head_size = width_here // heads_here
    block_rows = min(512, row_count)
    block_count = row_count // block_rows
    shape_blocks = (block_count, block_rows, heads_here, head_size)
    query_blocks = query_full.reshape(shape_blocks)
    key_blocks = key_full.reshape(shape_blocks)
    value_blocks = value_full.reshape(shape_blocks)
    offsets = jnp.arange(block_rows, dtype=jnp.float32)
    spacing = offsets[:, None] - offsets[None, :]
    inner_decay = jnp.where(spacing[None] >= 0, jnp.exp(-decay_rate[:, None, None] * jnp.maximum(spacing, 0.0)[None]), 0.0)
    query_decay = jnp.exp(-(offsets[:, None] + 1.0) * decay_rate[None, :])
    key_decay = jnp.exp(-(block_rows - 1.0 - offsets)[:, None] * decay_rate[None, :])
    block_decay = jnp.exp(-float(block_rows) * decay_rate)

    def advance(carry_state, pieces):
        query_part, key_part, value_part = pieces
        raw_scores = jnp.einsum('uhd,whd->huw', query_part, key_part, preferred_element_type=jnp.float32)
        weighted = (raw_scores * inner_decay).astype(jnp.bfloat16)
        within_block = jnp.einsum('huw,whe->uhe', weighted, value_part, preferred_element_type=jnp.float32)
        from_state = jnp.einsum('uhd,hde->uhe', query_part * query_decay[:, :, None], carry_state, precision=highest)
        carry_state = block_decay[:, None, None] * carry_state + jnp.einsum('whd,whe->hde', key_part * key_decay[:, :, None], value_part.astype(jnp.float32), precision=highest)
        return (carry_state, within_block + from_state)
    initial = jnp.zeros((heads_here, head_size, head_size), jnp.float32)
    unused, block_outputs = lax.scan(advance, initial, (query_blocks, key_blocks, value_blocks))
    local_out = block_outputs.reshape(row_count, width_here)
    positions = jnp.arange(row_count, dtype=jnp.float32)
    remaining = jnp.maximum(length.astype(jnp.float32) - 1.0 - positions, 0.0)
    key_end = jnp.exp(-remaining[:, None] * decay_rate[None, :])
    key_heads = key_full.reshape(row_count, heads_here, head_size)
    value_heads = value_full.reshape(row_count, heads_here, head_size)
    local_state = jnp.einsum('thd,the->hde', key_heads * key_end[:, :, None], value_heads.astype(jnp.float32), precision=highest)
    return (local_out, local_state)

def correction(query_full, carried, decay_rate):
    row_count, width_here = query_full.shape
    heads_here = decay_rate.shape[0]
    head_size = width_here // heads_here
    positions = jnp.arange(row_count, dtype=jnp.float32)
    query_scale = jnp.exp(-(positions[:, None] + 1.0) * decay_rate[None, :])
    query_heads = query_full.reshape(row_count, heads_here, head_size)
    result = jnp.einsum('thd,hde->the', query_heads * query_scale[:, :, None], carried, precision=highest)
    return result.reshape(row_count, width_here)

def reference(queries, key_tokens, values, upstream, norm_gain, decay_rate, block_length, parent):
    width = HEADS * DH
    weights = ancestry(block_length, parent, decay_rate)
    valid_mask = (jnp.arange(TOK_DEV)[None, :] < block_length[:, None])[:, :, None]

    def forward(query_in, key_in, value_in):
        query_full = jnp.where(valid_mask, query_in.reshape(BLOCKS, TOK_DEV, width), 0)
        key_full = jnp.where(valid_mask, key_in.reshape(BLOCKS, TOK_DEV, width), 0)
        value_full = jnp.where(valid_mask, value_in.reshape(BLOCKS, TOK_DEV, width), 0)

        def one_block(items):
            return block_local(items[0], items[1], items[2], items[3], decay_rate)
        local_out, local_state = lax.map(jax.checkpoint(one_block), (query_full, key_full, value_full, block_length))

        def carried_for(weight_row):
            return jnp.einsum('jh,jhde->hde', weight_row, local_state, precision=highest)
        carried = lax.map(carried_for, weights)

        def corrected(items):
            return correction(items[0], items[1], decay_rate)
        attended = (local_out + lax.map(corrected, (query_full, carried))).reshape(TOKENS, width)
        inverse = lax.rsqrt(lax.optimization_barrier(jnp.mean(attended * attended, axis=1)) + norm_eps)
        return (attended * inverse[:, None] * norm_gain[None, :]).astype(jnp.bfloat16)
    attention_out, pull = jax.vjp(forward, queries, key_tokens, values)
    query_grad, key_grad, value_grad = pull(upstream)
    return (attention_out, query_grad.astype(jnp.bfloat16), key_grad.astype(jnp.bfloat16), value_grad.astype(jnp.bfloat16))
```

```python
import functools

import jax
import jax.numpy as jnp
from jax import lax
from jax.experimental import pallas as pl
from jax.experimental.pallas import tpu as pltpu
from jax.sharding import PartitionSpec as P

F32 = jnp.float32
BF16 = jnp.bfloat16
norm_eps = 1e-05
highest = lax.Precision.HIGHEST
DH = 128
QUADS = ((0, 0), (1, 0), (1, 1))


def mm(a, b, ca, cb):
    return lax.dot_general(a, b, (((ca,), (cb,)), ((), ())), preferred_element_type=F32)


def split(x):
    hi = x.astype(BF16)
    return hi, (x - hi.astype(F32)).astype(BF16)


def rows_iota(rows, lanes, start=0):
    return (lax.broadcasted_iota(jnp.int32, (rows, lanes), 0) + start).astype(F32)


def kernel(
    n,
    nz,
    length_ref,
    parent_ref,
    rate_ref,
    gain_ref,
    q_hbm,
    k_hbm,
    v_hbm,
    u_hbm,
    out_hbm,
    dq_hbm,
    dk_hbm,
    dv_hbm,
    qm,
    km,
    vm,
    um,
    ob,
    dqb,
    dkb,
    dvb,
    sc,
    att,
    da,
    dec,
    wgt,
    state_out,
    state_in,
    carry_out,
    carry_in,
    grad_out,
    grad_in,
    back_out,
    back_in,
    zsend,
    zrecv,
    wmat,
    wmat_t,
    in_sem,
    out_sem,
    send_sem,
    recv_sem,
):
    me = lax.axis_index("seg")
    z = lax.axis_index("head")
    rows, feats = qm.shape
    heads = feats // DH
    half = rows // 2
    chunk = 128
    chunks = rows // chunk
    slab = state_out.shape[1]
    per_head = DH // slab
    width = float(feats * nz)

    loads = [
        pltpu.make_async_copy(src, dst, in_sem.at[i])
        for i, (src, dst) in enumerate(((k_hbm, km), (v_hbm, vm), (q_hbm, qm), (u_hbm, um)))
    ]
    for load in loads:
        load.start()

    barrier = pltpu.get_barrier_semaphore()

    def greet_seg(i, c):
        pl.semaphore_signal(
            barrier, inc=1, device_id=(lax.rem(me + i, n), z), device_id_type=pl.DeviceIdType.MESH
        )
        return c

    def greet_head(i, c):
        pl.semaphore_signal(
            barrier, inc=1, device_id=(me, lax.rem(z + i, nz)), device_id_type=pl.DeviceIdType.MESH
        )
        return c

    lax.fori_loop(1, n, greet_seg, 0)
    lax.fori_loop(1, nz, greet_head, 0)

    def exchange(src, dst, which):
        def send(i, c):
            peer = lax.rem(me + i, n)
            pltpu.make_async_remote_copy(
                src_ref=src.at[peer],
                dst_ref=dst.at[me],
                send_sem=send_sem.at[which],
                recv_sem=recv_sem.at[which],
                device_id=(peer, z),
                device_id_type=pl.DeviceIdType.MESH,
            ).start()
            return c

        lax.fori_loop(1, n, send, 0)
        dst[me] = src[me]

    def every(src, dst, which, count):
        return pltpu.make_async_remote_copy(
            src_ref=src.at[pl.ds(0, count)],
            dst_ref=dst.at[pl.ds(0, count)],
            send_sem=send_sem.at[which],
            recv_sem=recv_sem.at[which],
            device_id=(me, z),
            device_id_type=pl.DeviceIdType.MESH,
        )

    length = length_ref[me].astype(F32)
    rates = [rate_ref[h] for h in range(heads)]

    def key_end(h, start, count):
        t = rows_iota(count, DH, start)
        return jnp.exp(-rates[h] * jnp.maximum(length - 1.0 - t, 0.0))

    def query_scale(h, start, count):
        return jnp.exp(-rates[h] * (rows_iota(count, DH, start) + 1.0))

    loads[0].wait()
    loads[1].wait()
    for h in range(heads):
        lanes = slice(h * DH, (h + 1) * DH)
        total = None
        for i in range(2):
            part = slice(i * half, (i + 1) * half)
            used = rows_iota(half, DH, i * half) < length
            key = jnp.where(used, km[part, lanes].astype(F32), 0.0)
            value = jnp.where(used, vm[part, lanes].astype(F32), 0.0).astype(BF16)
            hi, lo = split(key * key_end(h, i * half, half))
            term = mm(hi, value, 0, 0) + mm(lo, value, 0, 0)
            total = term if total is None else total + term
            km[part, lanes] = key.astype(BF16)
            vm[part, lanes] = value
        state_out[h * per_head : (h + 1) * per_head] = total.reshape(per_head, slab, DH)

    pl.semaphore_wait(barrier, n - 1 + nz - 1)
    exchange(state_out, state_in, 0)

    own_rate = rate_ref[me // per_head]
    lane = lax.broadcasted_iota(jnp.int32, (1, DH), 1)
    wmat[...] = jnp.zeros_like(wmat)

    def tree_row(b, c):
        p = parent_ref[b]
        at = jnp.maximum(p, 0)
        gain = jnp.exp(jnp.full((1, DH), -own_rate * length_ref[at].astype(F32)))
        wmat[pl.ds(b, 1), :] = jnp.where(lane == p, 1.0, 0.0) + gain * wmat[pl.ds(at, 1), :]
        return c

    lax.fori_loop(1, n, tree_row, 0)
    wmat_t[...] = wmat[...].T

    loads[2].wait()
    loads[3].wait()
    sc[...] = um[...].astype(F32) * gain_ref[...]
    qm[...] = jnp.where(
        rows_iota(rows, feats) < length, qm[...].astype(F32), 0.0
    ).astype(BF16)

    def attend(h):
        lanes = slice(h * DH, (h + 1) * DH)
        for i, j in QUADS:
            up, low = slice(i * half, (i + 1) * half), slice(j * half, (j + 1) * half)
            raw = mm(qm[up, lanes], km[low, lanes], 1, 1)
            space = (
                lax.broadcasted_iota(jnp.int32, (half, half), 0)
                - lax.broadcasted_iota(jnp.int32, (half, half), 1)
                + (i - j) * half
            ).astype(F32)
            decay = jnp.where(space >= 0.0, jnp.exp(-rates[h] * jnp.maximum(space, 0.0)), 0.0)
            weighted = (raw * decay).astype(BF16)
            dec[h, up, low] = decay
            wgt[h, up, low] = weighted
            local = mm(weighted, vm[low, lanes], 1, 0)
            att[up, lanes] = local if j == 0 else att[up, lanes] + local

    def combine(src, dst, weights):
        flat = jnp.concatenate([src[:, r, :] for r in range(slab)], axis=1)
        result = jnp.dot(weights, flat, precision=highest, preferred_element_type=F32)
        for r in range(slab):
            dst[:, r, :] = result[:, r * DH : (r + 1) * DH]

    attend(0)
    every(state_out, state_in, 0, n - 1).wait_recv()
    combine(state_in, carry_out, wmat[0:n, 0:n])
    exchange(carry_out, carry_in, 1)
    for h in range(1, heads):
        attend(h)
    every(carry_out, carry_in, 1, n - 1).wait_recv()

    def carried(h):
        return carry_in[h * per_head : (h + 1) * per_head].reshape(DH, DH)

    for h in range(heads):
        lanes = slice(h * DH, (h + 1) * DH)
        hi, lo = split(carried(h))
        query = qm[:, lanes]
        att[:, lanes] += query_scale(h, 0, rows) * (mm(query, hi, 1, 0) + mm(query, lo, 1, 0))

    ones = jnp.ones((8, DH), BF16)
    row = lax.broadcasted_iota(jnp.int32, (8, DH), 0)
    message = jnp.zeros((8, DH), F32)
    for c in range(chunks):
        part = slice(c * chunk, (c + 1) * chunk)
        a, s = att[part, :], sc[part, :]
        for at, product in ((c, a * a), (chunks + c, a * s)):
            folded = product[:, :DH]
            for h in range(1, heads):
                folded = folded + product[:, h * DH : (h + 1) * DH]
            hi, lo = split(folded)
            message = jnp.where(row == at, mm(ones, hi, 1, 1) + mm(ones, lo, 1, 1), message)
    zsend[...] = message

    def send_sums(i, c):
        peer = lax.rem(z + i, nz)
        pltpu.make_async_remote_copy(
            src_ref=zsend,
            dst_ref=zrecv.at[z],
            send_sem=send_sem.at[4],
            recv_sem=recv_sem.at[4],
            device_id=(me, peer),
            device_id_type=pl.DeviceIdType.MESH,
        ).start()
        return c

    lax.fori_loop(1, nz, send_sums, 0)
    zrecv[z] = message
    every(zrecv, zrecv, 4, nz - 1).wait_recv()
    sums = jnp.sum(zrecv[...], axis=0)
    inverse = lax.rsqrt(sums / width + norm_eps)
    inner = pltpu.roll(sums, chunks, 0)
    slope = inverse * inverse * inverse * inner / width
    packed = jnp.where(row < chunks, inverse, pltpu.roll(slope, chunks, 0))
    columns = jnp.concatenate([packed] * (DH // 8), axis=0).T

    for c in range(chunks):
        part = slice(c * chunk, (c + 1) * chunk)
        da[part, :] = (
            columns[:, c : c + 1] * sc[part, :] - columns[:, chunks + c : chunks + c + 1] * att[part, :]
        )
    for h in range(heads):
        lanes = slice(h * DH, (h + 1) * DH)
        hi, lo = split(query_scale(h, 0, rows) * da[:, lanes])
        query = qm[:, lanes]
        grad = mm(query, hi, 0, 0) + mm(query, lo, 0, 0)
        grad_out[h * per_head : (h + 1) * per_head] = grad.reshape(per_head, slab, DH)
    exchange(grad_out, grad_in, 2)

    for c in range(chunks):
        part = slice(c * chunk, (c + 1) * chunk)
        ob[part, :] = (att[part, :] * columns[:, c : c + 1] * gain_ref[...]).astype(BF16)
    stores = [
        pltpu.make_async_copy(src, dst, out_sem.at[i])
        for i, (src, dst) in enumerate(((ob, out_hbm), (dqb, dq_hbm), (dkb, dk_hbm), (dvb, dv_hbm)))
    ]
    stores[0].start()

    def pull(h):
        lanes = slice(h * DH, (h + 1) * DH)
        dq = [None, None]
        dk = [None, None]
        dv = [None, None]

        def added(sums, at, term):
            sums[at] = term if sums[at] is None else sums[at] + term

        for i, j in QUADS:
            up, low = slice(i * half, (i + 1) * half), slice(j * half, (j + 1) * half)
            grad = da[up, lanes].astype(BF16)
            dweighted = mm(grad, vm[low, lanes], 1, 1).astype(BF16).astype(F32)
            draw = (dweighted * dec[h, up, low]).astype(BF16)
            added(dq, i, mm(draw, km[low, lanes], 1, 0))
            added(dk, j, mm(draw, qm[up, lanes], 0, 0))
            added(dv, j, mm(wgt[h, up, low], grad, 0, 0))
        chi, clo = split(carried(h))
        for i in range(2):
            part = slice(i * half, (i + 1) * half)
            ghi, glo = split(da[part, lanes])
            through = mm(ghi, chi, 1, 1) + mm(ghi, clo, 1, 1) + mm(glo, chi, 1, 1)
            through = (through * query_scale(h, i * half, half)).astype(BF16).astype(F32)
            both = dq[i].astype(BF16).astype(F32) + through
            used = rows_iota(half, DH, i * half) < length
            dqb[part, lanes] = jnp.where(used, both, 0.0).astype(BF16)
            dkb[part, lanes] = dk[i].astype(BF16)
            dvb[part, lanes] = dv[i].astype(BF16)

    pull(0)
    every(grad_out, grad_in, 2, n - 1).wait_recv()
    combine(grad_in, back_out, wmat_t[0:n, 0:n])
    exchange(back_out, back_in, 3)
    for h in range(1, heads):
        pull(h)
    stores[1].start()
    every(back_out, back_in, 3, n - 1).wait_recv()

    for h in range(heads):
        lanes = slice(h * DH, (h + 1) * DH)
        hi, lo = split(back_in[h * per_head : (h + 1) * per_head].reshape(DH, DH))
        for i in range(2):
            part = slice(i * half, (i + 1) * half)
            end = key_end(h, i * half, half)
            key, value = km[part, lanes], vm[part, lanes]
            dk = ((mm(value, hi, 1, 1) + mm(value, lo, 1, 1)) * end).astype(BF16).astype(F32)
            dv = ((mm(key, hi, 1, 0) + mm(key, lo, 1, 0)) * end).astype(BF16).astype(F32)
            dkb[part, lanes] = (dkb[part, lanes].astype(F32) + dk).astype(BF16)
            dvb[part, lanes] = (dvb[part, lanes].astype(F32) + dv).astype(BF16)
    stores[2].start()
    stores[3].start()
    for which, src in enumerate((state_out, carry_out, grad_out, back_out)):
        every(src, src, which, n - 1).wait_send()
    every(zrecv, zrecv, 4, nz - 1).wait_send()
    for store in stores:
        store.wait()


def solution(mesh):
    n, nz = mesh.shape["seg"], mesh.shape["head"]

    def local(queries, key_tokens, values, upstream, norm_gain, decay_rate, block_length, parent):
        rows, feats = queries.shape
        heads = feats // DH
        slab = feats // n
        anyspace = pl.BlockSpec(memory_space=pl.ANY)
        smem = pl.BlockSpec(memory_space=pltpu.SMEM)
        vmem = pl.BlockSpec(memory_space=pltpu.VMEM)
        tokens16 = pltpu.VMEM((rows, feats), BF16)
        tokens32 = pltpu.VMEM((rows, feats), F32)
        state = pltpu.VMEM((n, slab, DH), F32)
        return pl.pallas_call(
            functools.partial(kernel, n, nz),
            out_shape=[jax.ShapeDtypeStruct((rows, feats), BF16)] * 4,
            in_specs=[smem, smem, smem, vmem] + [anyspace] * 4,
            out_specs=[anyspace] * 4,
            scratch_shapes=[tokens16] * 8
            + [tokens32] * 3
            + [pltpu.VMEM((heads, rows, rows), F32), pltpu.VMEM((heads, rows, rows), BF16)]
            + [state] * 8
            + [pltpu.VMEM((8, DH), F32), pltpu.VMEM((nz, 8, DH), F32)]
            + [pltpu.VMEM((DH, DH), F32)] * 2
            + [
                pltpu.SemaphoreType.DMA((4,)),
                pltpu.SemaphoreType.DMA((4,)),
                pltpu.SemaphoreType.DMA((5,)),
                pltpu.SemaphoreType.DMA((5,)),
            ],
            compiler_params=pltpu.CompilerParams(
                collective_id=0, has_side_effects=True, vmem_limit_bytes=48 << 20
            ),
        )(
            block_length,
            parent,
            decay_rate,
            norm_gain.reshape(1, feats),
            queries,
            key_tokens,
            values,
            upstream,
        )

    tokens = P("seg", "head")
    return jax.shard_map(
        local,
        mesh=mesh,
        in_specs=(tokens, tokens, tokens, tokens, P("head"), P("head"), P(), P()),
        out_specs=(tokens,) * 4,
        check_vma=False,
    )
```

```python
import functools

import jax
import jax.numpy as jnp
from jax import lax
from jax.experimental import pallas as pl
from jax.experimental.pallas import tpu as pltpu
from jax.sharding import PartitionSpec as P

F32 = jnp.float32
BF16 = jnp.bfloat16
MESH = pl.DeviceIdType.MESH
norm_eps = 1e-05
DH = 128
QUADS = ((0, 0), (1, 0), (1, 1))


def mm(a, b, ca, cb):
    return lax.dot_general(a, b, (((ca,), (cb,)), ((), ())), preferred_element_type=F32)


def split(x):
    hi = x.astype(BF16)
    return hi, (x - hi.astype(F32)).astype(BF16)


def iota(shape, dim):
    return lax.broadcasted_iota(jnp.int32, shape, dim)


def seg_peers(me, n):
    if n != 32:
        return [lax.rem(me + i, n) for i in range(1, n)]
    y, x, core = me // 8, (me // 2) % 4, me % 2
    hops = (0, 1, 2, 1)
    steps = [(dy, dx, dc) for dy in range(4) for dx in range(4) for dc in range(2)]
    steps.sort(key=lambda s: -(hops[s[0]] + hops[s[1]]))
    return [
        ((y + dy) % 4) * 8 + ((x + dx) % 4) * 2 + (core + dc) % 2
        for dy, dx, dc in steps
        if (dy, dx, dc) != (0, 0, 0)
    ]


def head_peers(z, nz):
    steps = sorted(range(1, nz), key=lambda d: -min(d, nz - d))
    return [lax.rem(z + d, nz) for d in steps]


def kernel(
    n,
    nz,
    length_hbm,
    parent_hbm,
    rate_hbm,
    gain_hbm,
    q_hbm,
    k_hbm,
    v_hbm,
    u_hbm,
    ob,
    dqb,
    dkb,
    dvb,
    qm,
    km,
    vm,
    um,
    dab,
    sc,
    att,
    da,
    kscale,
    qscale,
    dkl,
    dvl,
    pair,
    qst,
    dec,
    wgt,
    state_out,
    state_in,
    carry_out,
    carry_in,
    grad_out,
    grad_in,
    back_out,
    back_in,
    zsend,
    zrecv,
    tree,
    tree_gain,
    whi,
    wlo,
    thi,
    tlo,
    length_ref,
    parent_ref,
    rate_ref,
    gain_ref,
    in_sem,
    send_sem,
    recv_sem,
    token,
):
    me = lax.axis_index("seg")
    z = lax.axis_index("head")
    rows, feats = qm.shape
    heads = feats // DH
    half = rows // 2
    chunk = DH
    chunks = rows // chunk
    slab = state_out.shape[1]
    per_head = DH // slab
    width = float(feats * nz)

    loads = [
        pltpu.make_async_copy(src, dst, in_sem.at[i])
        for i, (src, dst) in enumerate(
            (
                (k_hbm, km),
                (length_hbm, length_ref),
                (rate_hbm, rate_ref),
                (v_hbm, vm),
                (parent_hbm, parent_ref),
                (q_hbm, qm),
                (u_hbm, um),
                (gain_hbm, gain_ref),
            )
        )
    ]
    for load in loads:
        load.start()

    barrier = pltpu.get_barrier_semaphore()
    peers = seg_peers(me, n)
    lines = head_peers(z, nz)

    def greet(sem, peer):
        pl.semaphore_signal(sem, inc=1, device_id=peer, device_id_type=MESH)

    def along(step):
        return (me, lax.rem(z + step, nz)), (me, lax.rem(z + nz - step, nz))

    for peer in peers:
        greet(barrier, (peer, z))
    for peer in along(1):
        greet(barrier, peer)

    def exchange(src, dst, which):
        for peer in peers:
            pltpu.make_async_remote_copy(
                src_ref=src.at[peer],
                dst_ref=dst.at[me],
                send_sem=send_sem.at[which],
                recv_sem=recv_sem.at[which],
                device_id=(peer, z),
                device_id_type=MESH,
            ).start()
        dst[me] = src[me]

    def every(src, dst, which, count):
        return pltpu.make_async_remote_copy(
            src_ref=src.at[pl.ds(0, count)],
            dst_ref=dst.at[pl.ds(0, count)],
            send_sem=send_sem.at[which],
            recv_sem=recv_sem.at[which],
            device_id=(me, z),
            device_id_type=MESH,
        )

    for load in loads[:4]:
        load.wait()
    length = length_ref[me].astype(F32)
    rates = [rate_ref[h] for h in range(heads)]
    at_row = iota((1, rows), 1).astype(F32)
    for h in range(heads):
        lanes = slice(h * DH, (h + 1) * DH)
        end = jnp.where(at_row < length, jnp.exp(-rates[h] * (length - 1.0 - at_row)), 0.0)
        hi, lo = split(km[:, lanes].T.astype(F32) * end)
        total = mm(hi, vm[:, lanes], 1, 0) + mm(lo, vm[:, lanes], 1, 0)
        state_out[h * per_head : (h + 1) * per_head] = total.reshape(per_head, slab, DH)

    pl.semaphore_wait(barrier, n - 1 + 2)
    exchange(state_out, state_in, 0)
    for peer in along(1):
        greet(token.at[0], peer)

    for load in loads[4:]:
        load.wait()
    own_rate = rate_ref[me // per_head]
    place = jnp.where(
        iota((slab, feats), 1) % slab == iota((slab, feats), 0), iota((slab, feats), 1) // slab, -2
    )
    tree[pl.ds(0, slab), :] = jnp.zeros((slab, feats), F32)
    tree_gain[0] = jnp.zeros((slab, feats), F32)
    for b in range(1, n):
        p = parent_ref[b]
        branch = jnp.where(place == p, 1.0, 0.0) + tree_gain[jnp.maximum(p, 0)]
        tree[b * slab : (b + 1) * slab, :] = branch
        fade = jnp.exp(jnp.full((slab, feats), -own_rate * length_ref[b].astype(F32)))
        tree_gain[b] = branch * fade
    hi, lo = split(tree[...])
    whi[...] = hi
    wlo[...] = lo

    used = iota((rows, feats), 0).astype(F32) < length
    for ref in (qm, km, vm):
        ref[...] = jnp.where(used, ref[...].astype(F32), 0.0).astype(BF16)

    def attend(h):
        lanes = slice(h * DH, (h + 1) * DH)
        for i, j in QUADS:
            up, low = slice(i * half, (i + 1) * half), slice(j * half, (j + 1) * half)
            raw = mm(qm[up, lanes], km[low, lanes], 1, 1)
            space = (iota((half, half), 0) - iota((half, half), 1) + (i - j) * half).astype(F32)
            decay = jnp.where(space >= 0.0, jnp.exp(-rates[h] * jnp.maximum(space, 0.0)), 0.0)
            weighted = (raw * decay).astype(BF16)
            dec[h, up, low] = decay
            wgt[h, up, low] = weighted
            local = mm(weighted, vm[low, lanes], 1, 0)
            att[up, lanes] = local if j == 0 else att[up, lanes] + local

    def combine(src, dst, hi, lo):
        xhi, xlo = split(src[...].reshape(n * slab, DH))
        result = mm(hi[...], xhi, 1, 0) + mm(hi[...], xlo, 1, 0) + mm(lo[...], xhi, 1, 0)
        dst[...] = result.reshape(n, slab, DH)

    attend(0)
    pl.semaphore_wait(token.at[0], 2)
    for peer in along(2):
        greet(token.at[1], peer)
    every(state_out, state_in, 0, n - 1).wait_recv()
    combine(state_in, carry_out, whi, wlo)
    exchange(carry_out, carry_in, 1)

    for h in range(1, heads):
        attend(h)
    scaled = um[...].astype(F32) * gain_ref[...]
    sc[...] = scaled
    pair[0:rows, :] = scaled.astype(BF16)
    at_col = iota((rows, DH), 0).astype(F32)
    for h in range(heads):
        lanes = slice(h * DH, (h + 1) * DH)
        qscale[:, lanes] = jnp.exp(-rates[h] * (at_col + 1.0))
        kscale[:, lanes] = jnp.exp(-rates[h] * jnp.maximum(length - 1.0 - at_col, 0.0))
        qst[h] = qm[:, lanes].T.astype(F32) * jnp.exp(-rates[h] * (at_row + 1.0))
    hi, lo = split(tree[...].T)
    thi[...] = hi
    tlo[...] = lo
    pl.semaphore_wait(token.at[1], 2)
    for peer in along(4):
        greet(token.at[2], peer)
    every(carry_out, carry_in, 1, n - 1).wait_recv()

    def carried(h):
        return carry_in[h * per_head : (h + 1) * per_head].reshape(DH, DH)

    entering = [split(carried(h)) for h in range(heads)]
    ones = jnp.ones((8, DH), BF16)
    row = iota((8, DH), 0)
    message = jnp.zeros((8, DH), F32)
    for c in range(chunks):
        part = slice(c * chunk, (c + 1) * chunk)
        square = inner = None
        for h in range(heads):
            lanes = slice(h * DH, (h + 1) * DH)
            query = qm[part, lanes]
            brought = mm(query, entering[h][0], 1, 0) + mm(query, entering[h][1], 1, 0)
            a = att[part, lanes] + qscale[part, lanes] * brought
            att[part, lanes] = a
            pair[rows + c * chunk : rows + (c + 1) * chunk, lanes] = a.astype(BF16)
            square = a * a if square is None else square + a * a
            term = a * sc[part, lanes]
            inner = term if inner is None else inner + term
        message = jnp.where(row == c, mm(ones, square.astype(BF16), 1, 1), message)
        message = jnp.where(row == chunks + c, mm(ones, inner.astype(BF16), 1, 1), message)
    zsend[...] = message
    pl.semaphore_wait(token.at[2], 2)
    for peer in lines:
        pltpu.make_async_remote_copy(
            src_ref=zsend,
            dst_ref=zrecv.at[z],
            send_sem=send_sem.at[4],
            recv_sem=recv_sem.at[4],
            device_id=(me, peer),
            device_id_type=MESH,
        ).start()
    zrecv[z] = message
    every(zrecv, zrecv, 4, nz - 1).wait_recv()
    sums = jnp.sum(zrecv[...], axis=0)
    inverse = lax.rsqrt(sums / width + norm_eps)
    slope = inverse * inverse * inverse * pltpu.roll(sums, chunks, 0) / width

    for h in range(heads):
        lanes = slice(h * DH, (h + 1) * DH)
        parts = []
        for scalars in (inverse, -slope):
            for c in range(chunks):
                piece = qst[h, :, c * chunk : (c + 1) * chunk] * scalars[c : c + 1, :]
                parts.append(piece.astype(BF16))
        grad = mm(jnp.concatenate(parts, axis=1), pair[:, lanes], 1, 0)
        grad_out[h * per_head : (h + 1) * per_head] = grad.reshape(per_head, slab, DH)
    exchange(grad_out, grad_in, 2)

    packed = jnp.where(row < chunks, inverse, pltpu.roll(slope, chunks, 0))
    columns = jnp.concatenate([packed] * (DH // 8), axis=0).T
    for c in range(chunks):
        part = slice(c * chunk, (c + 1) * chunk)
        inv, bend = columns[:, c : c + 1], columns[:, chunks + c : chunks + c + 1]
        a = att[part, :]
        grad = inv * sc[part, :] - bend * a
        da[part, :] = grad
        dab[part, :] = grad.astype(BF16)
        ob[part, :] = (a * inv * gain_ref[...]).astype(BF16)
    def pull(h):
        lanes = slice(h * DH, (h + 1) * DH)
        dq = [None, None]
        dk = [None, None]
        dv = [None, None]

        def added(sums, at, term):
            sums[at] = term if sums[at] is None else sums[at] + term

        for i, j in QUADS:
            up, low = slice(i * half, (i + 1) * half), slice(j * half, (j + 1) * half)
            grad = dab[up, lanes]
            dweighted = mm(grad, vm[low, lanes], 1, 1).astype(BF16).astype(F32)
            draw = (dweighted * dec[h, up, low]).astype(BF16)
            added(dq, i, mm(draw, km[low, lanes], 1, 0))
            added(dk, j, mm(draw, qm[up, lanes], 0, 0))
            added(dv, j, mm(wgt[h, up, low], grad, 0, 0))
        chi, clo = split(carried(h))
        for i in range(2):
            part = slice(i * half, (i + 1) * half)
            ghi, glo = split(da[part, lanes])
            through = mm(ghi, chi, 1, 1) + mm(ghi, clo, 1, 1) + mm(glo, chi, 1, 1)
            total = dq[i] + through * qscale[part, lanes]
            inside = iota((half, DH), 0).astype(F32) < length - float(i * half)
            dqb[part, lanes] = jnp.where(inside, total, 0.0).astype(BF16)
            dkl[part, lanes] = dk[i]
            dvl[part, lanes] = dv[i]

    pull(0)
    every(grad_out, grad_in, 2, n - 1).wait_recv()
    combine(grad_in, back_out, thi, tlo)
    exchange(back_out, back_in, 3)
    for h in range(1, heads):
        pull(h)
    every(back_out, back_in, 3, n - 1).wait_recv()

    leaving = [
        split(back_in[h * per_head : (h + 1) * per_head].reshape(DH, DH)) for h in range(heads)
    ]
    for i in range(2):
        part = slice(i * half, (i + 1) * half)
        for h in range(heads):
            lanes = slice(h * DH, (h + 1) * DH)
            hi, lo = leaving[h]
            key, value, end = km[part, lanes], vm[part, lanes], kscale[part, lanes]
            dk = mm(value, hi, 1, 1) + mm(value, lo, 1, 1)
            dv = mm(key, hi, 1, 0) + mm(key, lo, 1, 0)
            dkb[part, lanes] = (dkl[part, lanes] + end * dk).astype(BF16)
            dvb[part, lanes] = (dvl[part, lanes] + end * dv).astype(BF16)
    for which, src in enumerate((state_out, carry_out, grad_out, back_out)):
        every(src, src, which, n - 1).wait_send()
    every(zrecv, zrecv, 4, nz - 1).wait_send()


def publish(*refs):
    count = (len(refs) - 1) // 2
    copies = [
        pltpu.make_async_copy(refs[i], refs[count + i], refs[-1].at[i]) for i in range(count)
    ]
    for copy in copies:
        copy.start()
    for copy in copies:
        copy.wait()


def solution(mesh):
    n, nz = mesh.shape["seg"], mesh.shape["head"]

    def local(queries, key_tokens, values, upstream, norm_gain, decay_rate, block_length, parent):
        rows, feats = queries.shape
        heads = feats // DH
        slab = feats // n
        hbm = pl.BlockSpec(memory_space=pltpu.HBM)
        vmem = pl.BlockSpec(memory_space=pltpu.VMEM)
        tokens16 = pltpu.VMEM((rows, feats), BF16)
        tokens32 = pltpu.VMEM((rows, feats), F32)
        state = pltpu.VMEM((n, slab, DH), F32)
        square32 = pltpu.VMEM((feats, feats), F32)
        square16 = pltpu.VMEM((feats, feats), BF16)
        result = pl.pallas_call(
            functools.partial(kernel, n, nz),
            out_shape=[tokens16] * 4,
            in_specs=[hbm] * 8,
            out_specs=[vmem] * 4,
            scratch_shapes=[tokens16] * 5
            + [tokens32] * 7
            + [pltpu.VMEM((2 * rows, feats), BF16), pltpu.VMEM((heads, DH, rows), F32)]
            + [pltpu.VMEM((heads, rows, rows), F32), pltpu.VMEM((heads, rows, rows), BF16)]
            + [state] * 8
            + [pltpu.VMEM((8, DH), F32), pltpu.VMEM((nz, 8, DH), F32)]
            + [square32, pltpu.VMEM((n, slab, feats), F32)]
            + [square16] * 4
            + [
                pltpu.SMEM((n,), jnp.int32),
                pltpu.SMEM((n,), jnp.int32),
                pltpu.SMEM((heads,), F32),
                pltpu.VMEM((1, feats), F32),
                pltpu.SemaphoreType.DMA((8,)),
                pltpu.SemaphoreType.DMA((5,)),
                pltpu.SemaphoreType.DMA((5,)),
                pltpu.SemaphoreType.REGULAR((3,)),
            ],
            compiler_params=pltpu.CompilerParams(
                collective_id=0, has_side_effects=True, vmem_limit_bytes=24 << 20
            ),
        )(
            *[
                pltpu.with_memory_space_constraint(x, pltpu.HBM)
                for x in (
                    block_length,
                    parent,
                    decay_rate,
                    norm_gain.reshape(1, feats),
                    queries,
                    key_tokens,
                    values,
                    upstream,
                )
            ]
        )
        return pl.pallas_call(
            publish,
            out_shape=[jax.ShapeDtypeStruct((rows, feats), BF16)] * 4,
            in_specs=[vmem] * 4,
            out_specs=[hbm] * 4,
            scratch_shapes=[pltpu.SemaphoreType.DMA((4,))],
            compiler_params=pltpu.CompilerParams(has_side_effects=True, vmem_limit_bytes=1 << 20),
        )(*[pltpu.with_memory_space_constraint(x, pltpu.VMEM) for x in result])

    tokens = P("seg", "head")
    return jax.shard_map(
        local,
        mesh=mesh,
        in_specs=(tokens, tokens, tokens, tokens, P("head"), P("head"), P(), P()),
        out_specs=(tokens,) * 4,
        check_vma=False,
    )
```

```python
import functools

import jax
import jax.numpy as jnp
from jax import lax
from jax.experimental import pallas as pl
from jax.experimental.pallas import tpu as pltpu
from jax.sharding import PartitionSpec as P

F32 = jnp.float32
BF16 = jnp.bfloat16
MESH = pl.DeviceIdType.MESH
norm_eps = 1e-05
DH = 128
QUADS = ((0, 0), (1, 0), (1, 1))


def mm(a, b, ca, cb):
    return lax.dot_general(a, b, (((ca,), (cb,)), ((), ())), preferred_element_type=F32)


def split(x):
    hi = x.astype(BF16)
    return hi, (x - hi.astype(F32)).astype(BF16)


def iota(shape, dim):
    return lax.broadcasted_iota(jnp.int32, shape, dim)


def chip_peers(chip, count):
    if count != 16:
        return [lax.rem(chip + i, count) for i in range(1, count)]
    y, x = chip // 4, chip % 4
    hops = (0, 1, 2, 1)
    steps = [(dy, dx) for dy in range(4) for dx in range(4)]
    steps.sort(key=lambda s: -(hops[s[0]] + hops[s[1]]))
    return [((y + dy) % 4) * 4 + (x + dx) % 4 for dy, dx in steps[:-1]]


def both(a, dim):
    return jnp.concatenate([a, a], axis=dim)


def diagonal(blocks):
    none = jnp.zeros_like(blocks[0])
    return jnp.concatenate(
        [
            jnp.concatenate([b if j == i else none for j in range(len(blocks))], axis=1)
            for i, b in enumerate(blocks)
        ],
        axis=0,
    )


def head_peers(z, nz):
    steps = sorted(range(1, nz), key=lambda d: -min(d, nz - d))
    return [lax.rem(z + d, nz) for d in steps]


def kernel(
    n,
    nz,
    length_hbm,
    parent_hbm,
    rate_hbm,
    gain_hbm,
    q_hbm,
    k_hbm,
    v_hbm,
    u_hbm,
    ob,
    dqb,
    dkb,
    dvb,
    qm,
    km,
    vm,
    um,
    dab,
    kend,
    vend,
    qfade,
    sc,
    att,
    da,
    qscale,
    dkl,
    dvl,
    pair,
    qst,
    dec,
    wgt,
    state_out,
    state_in,
    carry_out,
    carry_in,
    grad_out,
    grad_in,
    back_out,
    back_in,
    zsend,
    zrecv,
    scalars_ref,
    tree,
    tree_gain,
    whi,
    wlo,
    thi,
    tlo,
    length_ref,
    parent_ref,
    rate_ref,
    gain_ref,
    in_sem,
    send_sem,
    recv_sem,
    token,
):
    me = lax.axis_index("seg")
    z = lax.axis_index("head")
    rows, feats = qm.shape
    heads = feats // DH
    half = rows // 2
    chunk = DH
    chunks = rows // chunk
    slab = state_out.shape[1]
    per_head = DH // slab
    width = float(feats * nz)

    loads = [
        pltpu.make_async_copy(src, dst, in_sem.at[i])
        for i, (src, dst) in enumerate(
            (
                (k_hbm, km),
                (length_hbm, length_ref),
                (rate_hbm, rate_ref),
                (v_hbm, vm),
                (parent_hbm, parent_ref),
                (q_hbm, qm),
                (u_hbm, um),
                (gain_hbm, gain_ref),
            )
        )
    ]
    for load in loads:
        load.start()

    barrier = pltpu.get_barrier_semaphore()
    chip, core = me // heads, me % heads
    chips = chip_peers(chip, per_head)
    peers = [c * heads + h for c in chips for h in range(heads)]
    peers += [chip * heads + (core + h) % heads for h in range(1, heads)]
    lines = head_peers(z, nz)

    def greet(sem, peer):
        pl.semaphore_signal(sem, inc=1, device_id=peer, device_id_type=MESH)

    def along(step):
        return (me, lax.rem(z + step, nz)), (me, lax.rem(z + nz - step, nz))

    for peer in peers:
        greet(barrier, (peer, z))
    for peer in along(1):
        greet(barrier, peer)

    def push(src, dst, which, peer):
        pltpu.make_async_remote_copy(
            src_ref=src,
            dst_ref=dst,
            send_sem=send_sem.at[which],
            recv_sem=recv_sem.at[which],
            device_id=(peer, z),
            device_id_type=MESH,
        ).start()

    def scatter(src, dst, which, h):
        for c in chips:
            push(src.at[h * per_head + c], dst.at[me], which, c * heads + h)

    def scatter_near(src, dst, which):
        for step in range(1, heads):
            h = (core + step) % heads
            push(src.at[h * per_head + chip], dst.at[me], which, chip * heads + h)
        dst[me] = src[core * per_head + chip]

    def give_back(src, dst, which):
        slot = core * per_head + chip
        for peer in peers:
            push(src.at[peer], dst.at[slot], which, peer)
        dst[slot] = src[me]

    def every(src, dst, which, count):
        return pltpu.make_async_remote_copy(
            src_ref=src.at[pl.ds(0, count)],
            dst_ref=dst.at[pl.ds(0, count)],
            send_sem=send_sem.at[which],
            recv_sem=recv_sem.at[which],
            device_id=(me, z),
            device_id_type=MESH,
        )

    for load in loads[:4]:
        load.wait()
    length = length_ref[me].astype(F32)
    rates = [rate_ref[h] for h in range(heads)]
    at_row = iota((1, rows), 1).astype(F32)
    for h in range(heads):
        lanes = slice(h * DH, (h + 1) * DH)
        end = jnp.where(at_row < length, jnp.exp(-rates[h] * (length - 1.0 - at_row)), 0.0)
        hi, lo = split(km[:, lanes].T.astype(F32) * end)
        stacked = mm(jnp.concatenate([hi, lo], axis=0), vm[:, lanes], 1, 0)
        total = stacked[:DH] + stacked[DH:]
        state_out[h * per_head : (h + 1) * per_head] = total.reshape(per_head, slab, DH)

    pl.semaphore_wait(barrier, n - 1 + 2)
    for h in range(heads):
        scatter(state_out, state_in, 0, h)
    scatter_near(state_out, state_in, 0)
    for peer in along(1):
        greet(token.at[0], peer)

    for load in loads[4:]:
        load.wait()
    own_rate = rate_ref[core]
    place = jnp.where(
        iota((slab, feats), 1) % slab == iota((slab, feats), 0), iota((slab, feats), 1) // slab, -2
    )
    tree[pl.ds(0, slab), :] = jnp.zeros((slab, feats), F32)
    tree_gain[0] = jnp.zeros((slab, feats), F32)
    for b in range(1, n):
        p = parent_ref[b]
        branch = jnp.where(place == p, 1.0, 0.0) + tree_gain[jnp.maximum(p, 0)]
        tree[b * slab : (b + 1) * slab, :] = branch
        fade = jnp.exp(jnp.full((slab, feats), -own_rate * length_ref[b].astype(F32)))
        tree_gain[b] = branch * fade
    hi, lo = split(tree[...])
    whi[...] = hi
    wlo[...] = lo

    used = iota((rows, feats), 0).astype(F32) < length
    for ref in (qm, km, vm):
        ref[...] = jnp.where(used, ref[...].astype(F32), 0.0).astype(BF16)

    def attend(h):
        lanes = slice(h * DH, (h + 1) * DH)
        for i, j in QUADS:
            up, low = slice(i * half, (i + 1) * half), slice(j * half, (j + 1) * half)
            raw = mm(qm[up, lanes], km[low, lanes], 1, 1)
            space = (iota((half, half), 0) - iota((half, half), 1) + (i - j) * half).astype(F32)
            decay = jnp.where(space >= 0.0, jnp.exp(-rates[h] * jnp.maximum(space, 0.0)), 0.0)
            weighted = (raw * decay).astype(BF16)
            dec[h, up, low] = decay
            wgt[h, up, low] = weighted
            local = mm(weighted, vm[low, lanes], 1, 0)
            att[up, lanes] = local if j == 0 else att[up, lanes] + local

    def combine(src, dst, hi, lo):
        xhi, xlo = split(src[...].reshape(n * slab, DH))
        wide = mm(hi[...], jnp.concatenate([xhi, xlo], axis=1), 1, 0)
        result = wide[:, :DH] + wide[:, DH:] + mm(lo[...], xhi, 1, 0)
        dst[...] = result.reshape(n, slab, DH)

    attend(0)
    pl.semaphore_wait(token.at[0], 2)
    for peer in along(2):
        greet(token.at[1], peer)
    every(state_out, state_in, 0, n - 1).wait_recv()
    combine(state_in, carry_out, whi, wlo)
    give_back(carry_out, carry_in, 1)

    for h in range(1, heads):
        attend(h)
    scaled = um[...].astype(F32) * gain_ref[...]
    sc[...] = scaled
    pair[0:rows, :] = scaled.astype(BF16)
    at_col = iota((rows, DH), 0).astype(F32)
    for h in range(heads):
        lanes = slice(h * DH, (h + 1) * DH)
        fade = jnp.exp(-rates[h] * (at_col + 1.0))
        qscale[:, lanes] = fade
        qfade[:, lanes] = (qm[:, lanes].astype(F32) * fade).astype(BF16)
        end = jnp.exp(-rates[h] * jnp.maximum(length - 1.0 - at_col, 0.0))
        kend[:, lanes] = (km[:, lanes].astype(F32) * end).astype(BF16)
        vend[:, lanes] = (vm[:, lanes].astype(F32) * end).astype(BF16)
        qst[h] = qm[:, lanes].T.astype(F32) * jnp.exp(-rates[h] * (at_row + 1.0))
    hi, lo = split(tree[...].T)
    thi[...] = hi
    tlo[...] = lo
    pl.semaphore_wait(token.at[1], 2)
    for peer in along(4):
        greet(token.at[2], peer)
    every(carry_out, carry_in, 1, n - 1).wait_recv()

    def carried(h):
        return carry_in[h * per_head : (h + 1) * per_head].reshape(DH, DH)

    entering = diagonal([carried(h).astype(BF16) for h in range(heads)])
    brought = mm(qfade[...], entering, 1, 0)
    ones = jnp.ones((8, DH), BF16)
    row = iota((8, DH), 0)
    message = jnp.zeros((8, DH), F32)
    for c in range(chunks):
        part = slice(c * chunk, (c + 1) * chunk)
        a = att[part, :] + brought[part]
        att[part, :] = a
        pair[rows + c * chunk : rows + (c + 1) * chunk, :] = a.astype(BF16)
        square, inner = a * a, a * sc[part, :]
        square = sum(square[:, h * DH : (h + 1) * DH] for h in range(heads))
        inner = sum(inner[:, h * DH : (h + 1) * DH] for h in range(heads))
        message = jnp.where(row == c, mm(ones, square.astype(BF16), 1, 1), message)
        message = jnp.where(row == chunks + c, mm(ones, inner.astype(BF16), 1, 1), message)
    zsend[...] = message
    pl.semaphore_wait(token.at[2], 2)
    for peer in lines:
        pltpu.make_async_remote_copy(
            src_ref=zsend,
            dst_ref=zrecv.at[z],
            send_sem=send_sem.at[4],
            recv_sem=recv_sem.at[4],
            device_id=(me, peer),
            device_id_type=MESH,
        ).start()
    zrecv[z] = message
    every(zrecv, zrecv, 4, nz - 1).wait_recv()
    sums = jnp.sum(zrecv[...], axis=0)
    inverse = lax.rsqrt(sums / width + norm_eps)
    slope = inverse * inverse * inverse * pltpu.roll(sums, chunks, 0) / width

    for h in range(heads):
        lanes = slice(h * DH, (h + 1) * DH)
        parts = []
        for scalars in (inverse, -slope):
            for c in range(chunks):
                piece = qst[h, :, c * chunk : (c + 1) * chunk] * scalars[c : c + 1, :]
                parts.append(piece.astype(BF16))
        grad = mm(jnp.concatenate(parts, axis=1), pair[:, lanes], 1, 0)
        grad_out[h * per_head : (h + 1) * per_head] = grad.reshape(per_head, slab, DH)
        scatter(grad_out, grad_in, 2, h)
    scatter_near(grad_out, grad_in, 2)

    scalars_ref[...] = jnp.where(row < chunks, inverse, pltpu.roll(slope, chunks, 0))

    def local_gradients():
        columns = jnp.concatenate([scalars_ref[...]] * (DH // 8), axis=0).T
        for c in range(chunks):
            part = slice(c * chunk, (c + 1) * chunk)
            inv, bend = columns[:, c : c + 1], columns[:, chunks + c : chunks + c + 1]
            a = att[part, :]
            grad = inv * sc[part, :] - bend * a
            da[part, :] = grad
            dab[part, :] = grad.astype(BF16)
            ob[part, :] = (a * inv * gain_ref[...]).astype(BF16)

    def pull(h):
        lanes = slice(h * DH, (h + 1) * DH)
        dq = [None, None]
        dk = [None, None]
        dv = [None, None]

        def added(sums, at, term):
            sums[at] = term if sums[at] is None else sums[at] + term

        for i, j in QUADS:
            up, low = slice(i * half, (i + 1) * half), slice(j * half, (j + 1) * half)
            grad = dab[up, lanes]
            dweighted = mm(grad, vm[low, lanes], 1, 1).astype(BF16).astype(F32)
            draw = (dweighted * dec[h, up, low]).astype(BF16)
            added(dq, i, mm(draw, km[low, lanes], 1, 0))
            added(dk, j, mm(draw, qm[up, lanes], 0, 0))
            added(dv, j, mm(wgt[h, up, low], grad, 0, 0))
        chi, clo = split(carried(h))
        for i in range(2):
            part = slice(i * half, (i + 1) * half)
            ghi, glo = split(da[part, lanes])
            through = mm(both(ghi, 1), jnp.concatenate([chi, clo], axis=1), 1, 1) + mm(glo, chi, 1, 1)
            total = dq[i] + through * qscale[part, lanes]
            inside = iota((half, DH), 0).astype(F32) < length - float(i * half)
            dqb[part, lanes] = jnp.where(inside, total, 0.0).astype(BF16)
            dkl[part, lanes] = dk[i]
            dvl[part, lanes] = dv[i]

    @pl.when(me >= 0)
    def _():
        local_gradients()
        pull(0)

    every(grad_out, grad_in, 2, n - 1).wait_recv()
    combine(grad_in, back_out, thi, tlo)
    give_back(back_out, back_in, 3)
    for h in range(1, heads):
        pull(h)
    every(back_out, back_in, 3, n - 1).wait_recv()

    leaving = diagonal(
        [
            back_in[h * per_head : (h + 1) * per_head].reshape(DH, DH).astype(BF16)
            for h in range(heads)
        ]
    )
    dkb[...] = (dkl[...] + mm(vend[...], leaving, 1, 1)).astype(BF16)
    dvb[...] = (dvl[...] + mm(kend[...], leaving, 1, 0)).astype(BF16)
    for which, src in enumerate((state_out, carry_out, grad_out, back_out)):
        every(src, src, which, n - 1).wait_send()
    every(zrecv, zrecv, 4, nz - 1).wait_send()


def publish(*refs):
    count = (len(refs) - 1) // 2
    copies = [
        pltpu.make_async_copy(refs[i], refs[count + i], refs[-1].at[i]) for i in range(count)
    ]
    for copy in copies:
        copy.start()
    for copy in copies:
        copy.wait()


def solution(mesh):
    n, nz = mesh.shape["seg"], mesh.shape["head"]

    def local(queries, key_tokens, values, upstream, norm_gain, decay_rate, block_length, parent):
        rows, feats = queries.shape
        heads = feats // DH
        slab = feats // n
        hbm = pl.BlockSpec(memory_space=pltpu.HBM)
        vmem = pl.BlockSpec(memory_space=pltpu.VMEM)
        tokens16 = pltpu.VMEM((rows, feats), BF16)
        tokens32 = pltpu.VMEM((rows, feats), F32)
        state = pltpu.VMEM((n, slab, DH), F32)
        square32 = pltpu.VMEM((feats, feats), F32)
        square16 = pltpu.VMEM((feats, feats), BF16)
        result = pl.pallas_call(
            functools.partial(kernel, n, nz),
            out_shape=[tokens16] * 4,
            in_specs=[hbm] * 8,
            out_specs=[vmem] * 4,
            scratch_shapes=[tokens16] * 8
            + [tokens32] * 6
            + [pltpu.VMEM((2 * rows, feats), BF16), pltpu.VMEM((heads, DH, rows), F32)]
            + [pltpu.VMEM((heads, rows, rows), F32), pltpu.VMEM((heads, rows, rows), BF16)]
            + [state] * 8
            + [pltpu.VMEM((8, DH), F32), pltpu.VMEM((nz, 8, DH), F32), pltpu.VMEM((8, DH), F32)]
            + [square32, pltpu.VMEM((n, slab, feats), F32)]
            + [square16] * 4
            + [
                pltpu.SMEM((n,), jnp.int32),
                pltpu.SMEM((n,), jnp.int32),
                pltpu.SMEM((heads,), F32),
                pltpu.VMEM((1, feats), F32),
                pltpu.SemaphoreType.DMA((8,)),
                pltpu.SemaphoreType.DMA((5,)),
                pltpu.SemaphoreType.DMA((5,)),
                pltpu.SemaphoreType.REGULAR((3,)),
            ],
            compiler_params=pltpu.CompilerParams(
                collective_id=0, has_side_effects=True, vmem_limit_bytes=24 << 20
            ),
        )(
            *[
                pltpu.with_memory_space_constraint(x, pltpu.HBM)
                for x in (
                    block_length,
                    parent,
                    decay_rate,
                    norm_gain.reshape(1, feats),
                    queries,
                    key_tokens,
                    values,
                    upstream,
                )
            ]
        )
        return pl.pallas_call(
            publish,
            out_shape=[jax.ShapeDtypeStruct((rows, feats), BF16)] * 4,
            in_specs=[vmem] * 4,
            out_specs=[hbm] * 4,
            scratch_shapes=[pltpu.SemaphoreType.DMA((4,))],
            compiler_params=pltpu.CompilerParams(has_side_effects=True, vmem_limit_bytes=1 << 20),
        )(*[pltpu.with_memory_space_constraint(x, pltpu.VMEM) for x in result])

    tokens = P("seg", "head")
    return jax.shard_map(
        local,
        mesh=mesh,
        in_specs=(tokens, tokens, tokens, tokens, P("head"), P("head"), P(), P()),
        out_specs=(tokens,) * 4,
        check_vma=False,
    )
```

```python
import functools

import jax
import jax.numpy as jnp
from jax import lax
from jax.experimental import pallas as pl
from jax.experimental.pallas import tpu as pltpu
from jax.sharding import PartitionSpec as P

F32 = jnp.float32
BF16 = jnp.bfloat16
MESH = pl.DeviceIdType.MESH
norm_eps = 1e-05
DH = 128
QUADS = ((0, 0), (1, 0), (1, 1))


def mm(a, b, ca, cb):
    return lax.dot_general(a, b, (((ca,), (cb,)), ((), ())), preferred_element_type=F32)


def split(x):
    hi = x.astype(BF16)
    return hi, (x - hi.astype(F32)).astype(BF16)


def iota(shape, dim):
    return lax.broadcasted_iota(jnp.int32, shape, dim)


def chip_peers(chip, count):
    if count != 16:
        return [lax.rem(chip + i, count) for i in range(1, count)]
    y, x = lax.div(chip, 4), lax.rem(chip, 4)
    ys = [lax.rem(y + d, 4) * 4 for d in range(4)]
    xs = [lax.rem(x + d, 4) for d in range(4)]
    hops = (0, 1, 2, 1)
    steps = [(dy, dx) for dy in range(4) for dx in range(4)]
    steps.sort(key=lambda s: -(hops[s[0]] + hops[s[1]]))
    return [ys[dy] + xs[dx] for dy, dx in steps[:-1]]


def both(a, dim):
    return jnp.concatenate([a, a], axis=dim)


def diagonal(blocks):
    none = jnp.zeros_like(blocks[0])
    return jnp.concatenate(
        [
            jnp.concatenate([b if j == i else none for j in range(len(blocks))], axis=1)
            for i, b in enumerate(blocks)
        ],
        axis=0,
    )


def head_peers(z, nz):
    steps = sorted(range(1, nz), key=lambda d: -min(d, nz - d))
    return [lax.rem(z + d, nz) for d in steps]


def kernel(
    n,
    nz,
    length_hbm,
    parent_hbm,
    rate_hbm,
    gain_hbm,
    q_hbm,
    k_hbm,
    v_hbm,
    u_hbm,
    ob,
    dqb,
    dkb,
    dvb,
    qm,
    km,
    vm,
    um,
    dab,
    kend,
    vend,
    qfade,
    sc,
    att,
    da,
    qscale,
    dkl,
    dvl,
    pair,
    qst,
    dec,
    wgt,
    state_out,
    state_in,
    carry_out,
    carry_in,
    grad_out,
    grad_in,
    back_out,
    back_in,
    zsend,
    zrecv,
    scalars_ref,
    tree,
    tree_gain,
    whi,
    wlo,
    thi,
    tlo,
    length_ref,
    parent_ref,
    rate_ref,
    gain_ref,
    in_sem,
    send_sem,
    recv_sem,
    token,
):
    me = lax.axis_index("seg")
    z = lax.axis_index("head")
    rows, feats = qm.shape
    heads = feats // DH
    half = rows // 2
    chunk = DH
    chunks = rows // chunk
    slab = state_out.shape[1]
    per_head = DH // slab
    width = float(feats * nz)

    loads = [
        pltpu.make_async_copy(src, dst, in_sem.at[i])
        for i, (src, dst) in enumerate(
            (
                (k_hbm, km),
                (length_hbm, length_ref),
                (rate_hbm, rate_ref),
                (v_hbm, vm),
                (parent_hbm, parent_ref),
                (q_hbm, qm),
                (u_hbm, um),
                (gain_hbm, gain_ref),
            )
        )
    ]
    for load in loads:
        load.start()

    barrier = pltpu.get_barrier_semaphore()
    chip, core = lax.div(me, heads), lax.rem(me, heads)
    chips = chip_peers(chip, per_head)
    peers = [c * heads + h for c in chips for h in range(heads)]
    peers += [chip * heads + lax.rem(core + h, heads) for h in range(1, heads)]
    lines = head_peers(z, nz)

    def greet(sem, peer):
        pl.semaphore_signal(sem, inc=1, device_id=peer, device_id_type=MESH)

    def along(step):
        return (me, lax.rem(z + step, nz)), (me, lax.rem(z + nz - step, nz))

    for peer in peers:
        greet(barrier, (peer, z))
    for peer in along(1):
        greet(barrier, peer)

    def push(src, dst, which, peer):
        pltpu.make_async_remote_copy(
            src_ref=src,
            dst_ref=dst,
            send_sem=send_sem.at[which],
            recv_sem=recv_sem.at[which],
            device_id=(peer, z),
            device_id_type=MESH,
        ).start()

    def scatter(src, dst, which, h):
        for c in chips:
            push(src.at[h * per_head + c], dst.at[me], which, c * heads + h)

    def scatter_near(src, dst, which):
        for step in range(1, heads):
            h = lax.rem(core + step, heads)
            push(src.at[h * per_head + chip], dst.at[me], which, chip * heads + h)
        dst[me] = src[core * per_head + chip]

    def give_back(src, dst, which):
        slot = core * per_head + chip
        for peer in peers:
            push(src.at[peer], dst.at[slot], which, peer)
        dst[slot] = src[me]

    def every(src, dst, which, count):
        return pltpu.make_async_remote_copy(
            src_ref=src.at[pl.ds(0, count)],
            dst_ref=dst.at[pl.ds(0, count)],
            send_sem=send_sem.at[which],
            recv_sem=recv_sem.at[which],
            device_id=(me, z),
            device_id_type=MESH,
        )

    for load in loads[:4]:
        load.wait()
    length = length_ref[me].astype(F32)
    rates = [rate_ref[h] for h in range(heads)]
    at_row = iota((1, rows), 1).astype(F32)
    for h in range(heads):
        lanes = slice(h * DH, (h + 1) * DH)
        end = jnp.where(at_row < length, jnp.exp(-rates[h] * (length - 1.0 - at_row)), 0.0)
        hi, lo = split(km[:, lanes].T.astype(F32) * end)
        stacked = mm(jnp.concatenate([hi, lo], axis=0), vm[:, lanes], 1, 0)
        total = stacked[:DH] + stacked[DH:]
        state_out[h * per_head : (h + 1) * per_head] = total.reshape(per_head, slab, DH)

    pl.semaphore_wait(barrier, n - 1 + 2)
    for h in range(heads):
        scatter(state_out, state_in, 0, h)
    scatter_near(state_out, state_in, 0)
    for peer in along(1):
        greet(token.at[0], peer)

    for load in loads[4:]:
        load.wait()
    own_rate = rate_ref[core]
    place = jnp.where(
        iota((slab, feats), 1) % slab == iota((slab, feats), 0), iota((slab, feats), 1) // slab, -2
    )
    tree[pl.ds(0, slab), :] = jnp.zeros((slab, feats), F32)
    tree_gain[0] = jnp.zeros((slab, feats), F32)
    for b in range(1, n):
        p = parent_ref[b]
        branch = jnp.where(place == p, 1.0, 0.0) + tree_gain[jnp.maximum(p, 0)]
        tree[b * slab : (b + 1) * slab, :] = branch
        fade = jnp.exp(jnp.full((slab, feats), -own_rate * length_ref[b].astype(F32)))
        tree_gain[b] = branch * fade
    hi, lo = split(tree[...])
    whi[...] = hi
    wlo[...] = lo

    used = iota((rows, feats), 0).astype(F32) < length
    for ref in (qm, km, vm):
        ref[...] = jnp.where(used, ref[...].astype(F32), 0.0).astype(BF16)

    def attend(h):
        lanes = slice(h * DH, (h + 1) * DH)
        for i, j in QUADS:
            up, low = slice(i * half, (i + 1) * half), slice(j * half, (j + 1) * half)
            raw = mm(qm[up, lanes], km[low, lanes], 1, 1)
            space = (iota((half, half), 0) - iota((half, half), 1) + (i - j) * half).astype(F32)
            decay = jnp.where(space >= 0.0, jnp.exp(-rates[h] * jnp.maximum(space, 0.0)), 0.0)
            weighted = (raw * decay).astype(BF16)
            dec[h, up, low] = decay
            wgt[h, up, low] = weighted
            local = mm(weighted, vm[low, lanes], 1, 0)
            att[up, lanes] = local if j == 0 else att[up, lanes] + local

    def combine(src, dst, hi, lo):
        x = src[...].reshape(n * slab, DH).astype(BF16)
        result = mm(jnp.concatenate([hi[...], lo[...]], axis=1), both(x, 0), 1, 0)
        dst[...] = result.reshape(n, slab, DH)

    attend(0)
    pl.semaphore_wait(token.at[0], 2)
    for peer in along(2):
        greet(token.at[1], peer)
    every(state_out, state_in, 0, n - 1).wait_recv()
    combine(state_in, carry_out, whi, wlo)
    give_back(carry_out, carry_in, 1)

    for h in range(1, heads):
        attend(h)
    scaled = um[...].astype(F32) * gain_ref[...]
    sc[...] = scaled
    pair[0:rows, :] = scaled.astype(BF16)
    at_col = iota((rows, DH), 0).astype(F32)
    for h in range(heads):
        lanes = slice(h * DH, (h + 1) * DH)
        fade = jnp.exp(-rates[h] * (at_col + 1.0))
        qscale[:, lanes] = fade
        qfade[:, lanes] = (qm[:, lanes].astype(F32) * fade).astype(BF16)
        end = jnp.exp(-rates[h] * jnp.maximum(length - 1.0 - at_col, 0.0))
        kend[:, lanes] = (km[:, lanes].astype(F32) * end).astype(BF16)
        vend[:, lanes] = (vm[:, lanes].astype(F32) * end).astype(BF16)
        qst[h] = qm[:, lanes].T.astype(F32) * jnp.exp(-rates[h] * (at_row + 1.0))
    hi, lo = split(tree[...].T)
    thi[...] = hi
    tlo[...] = lo
    pl.semaphore_wait(token.at[1], 2)
    for peer in along(4):
        greet(token.at[2], peer)
    every(carry_out, carry_in, 1, n - 1).wait_recv()

    def carried(h):
        return carry_in[h * per_head : (h + 1) * per_head].reshape(DH, DH)

    entering = diagonal([carried(h).astype(BF16) for h in range(heads)])
    brought = mm(qfade[...], entering, 1, 0)
    row = iota((8, DH), 0)
    block = iota((8, 2 * chunks * DH), 1) // DH
    chosen = iota((8, 2 * chunks * DH), 0) == block // 2 + (block % 2) * chunks
    folded = []
    for c in range(chunks):
        part = slice(c * chunk, (c + 1) * chunk)
        a = att[part, :] + brought[part]
        att[part, :] = a
        pair[rows + c * chunk : rows + (c + 1) * chunk, :] = a.astype(BF16)
        square, inner = a * a, a * sc[part, :]
        square = sum(square[:, h * DH : (h + 1) * DH] for h in range(heads))
        inner = sum(inner[:, h * DH : (h + 1) * DH] for h in range(heads))
        folded += [square.astype(BF16), inner.astype(BF16)]
    pick = jnp.where(chosen, 1.0, 0.0).astype(BF16)
    message = mm(pick, jnp.concatenate(folded, axis=1), 1, 1)
    zsend[...] = message
    pl.semaphore_wait(token.at[2], 2)
    for peer in lines:
        pltpu.make_async_remote_copy(
            src_ref=zsend,
            dst_ref=zrecv.at[z],
            send_sem=send_sem.at[4],
            recv_sem=recv_sem.at[4],
            device_id=(me, peer),
            device_id_type=MESH,
        ).start()
    zrecv[z] = message
    every(zrecv, zrecv, 4, nz - 1).wait_recv()
    sums = jnp.sum(zrecv[...], axis=0)
    inverse = lax.rsqrt(sums / width + norm_eps)
    slope = inverse * inverse * inverse * pltpu.roll(sums, chunks, 0) / width

    for h in range(heads):
        lanes = slice(h * DH, (h + 1) * DH)
        parts = []
        for scalars in (inverse, -slope):
            for c in range(chunks):
                piece = qst[h, :, c * chunk : (c + 1) * chunk] * scalars[c : c + 1, :]
                parts.append(piece.astype(BF16))
        grad = mm(jnp.concatenate(parts, axis=1), pair[:, lanes], 1, 0)
        grad_out[h * per_head : (h + 1) * per_head] = grad.reshape(per_head, slab, DH)
        scatter(grad_out, grad_in, 2, h)
    scatter_near(grad_out, grad_in, 2)

    scalars_ref[...] = jnp.where(row < chunks, inverse, pltpu.roll(slope, chunks, 0))

    def local_gradients():
        columns = jnp.concatenate([scalars_ref[...]] * (DH // 8), axis=0).T
        for c in range(chunks):
            part = slice(c * chunk, (c + 1) * chunk)
            inv, bend = columns[:, c : c + 1], columns[:, chunks + c : chunks + c + 1]
            a = att[part, :]
            grad = inv * sc[part, :] - bend * a
            da[part, :] = grad
            dab[part, :] = grad.astype(BF16)
            ob[part, :] = (a * inv * gain_ref[...]).astype(BF16)

    def pull(h):
        lanes = slice(h * DH, (h + 1) * DH)
        dq = [None, None]
        dk = [None, None]
        dv = [None, None]

        def added(sums, at, term):
            sums[at] = term if sums[at] is None else sums[at] + term

        for i, j in QUADS:
            up, low = slice(i * half, (i + 1) * half), slice(j * half, (j + 1) * half)
            grad = dab[up, lanes]
            dweighted = mm(grad, vm[low, lanes], 1, 1).astype(BF16).astype(F32)
            draw = (dweighted * dec[h, up, low]).astype(BF16)
            added(dq, i, mm(draw, km[low, lanes], 1, 0))
            added(dk, j, mm(draw, qm[up, lanes], 0, 0))
            added(dv, j, mm(wgt[h, up, low], grad, 0, 0))
        chi, clo = split(carried(h))
        for i in range(2):
            part = slice(i * half, (i + 1) * half)
            ghi, glo = split(da[part, lanes])
            through = mm(both(ghi, 1), jnp.concatenate([chi, clo], axis=1), 1, 1) + mm(glo, chi, 1, 1)
            total = dq[i] + through * qscale[part, lanes]
            inside = iota((half, DH), 0).astype(F32) < length - float(i * half)
            dqb[part, lanes] = jnp.where(inside, total, 0.0).astype(BF16)
            dkl[part, lanes] = dk[i]
            dvl[part, lanes] = dv[i]

    @pl.when(me >= 0)
    def _():
        local_gradients()
        pull(0)

    every(grad_out, grad_in, 2, n - 1).wait_recv()
    combine(grad_in, back_out, thi, tlo)
    give_back(back_out, back_in, 3)
    for h in range(1, heads):
        pull(h)
    every(back_out, back_in, 3, n - 1).wait_recv()

    leaving = diagonal(
        [
            back_in[h * per_head : (h + 1) * per_head].reshape(DH, DH).astype(BF16)
            for h in range(heads)
        ]
    )
    dkb[...] = (dkl[...] + mm(vend[...], leaving, 1, 1)).astype(BF16)
    dvb[...] = (dvl[...] + mm(kend[...], leaving, 1, 0)).astype(BF16)
    for which, src in enumerate((state_out, carry_out, grad_out, back_out)):
        every(src, src, which, n - 1).wait_send()
    every(zrecv, zrecv, 4, nz - 1).wait_send()


def publish(*refs):
    count = (len(refs) - 1) // 2
    copies = [
        pltpu.make_async_copy(refs[i], refs[count + i], refs[-1].at[i]) for i in range(count)
    ]
    for copy in copies:
        copy.start()
    for copy in copies:
        copy.wait()


def solution(mesh):
    n, nz = mesh.shape["seg"], mesh.shape["head"]

    def local(queries, key_tokens, values, upstream, norm_gain, decay_rate, block_length, parent):
        rows, feats = queries.shape
        heads = feats // DH
        slab = feats // n
        hbm = pl.BlockSpec(memory_space=pltpu.HBM)
        vmem = pl.BlockSpec(memory_space=pltpu.VMEM)
        tokens16 = pltpu.VMEM((rows, feats), BF16)
        tokens32 = pltpu.VMEM((rows, feats), F32)
        state = pltpu.VMEM((n, slab, DH), F32)
        square32 = pltpu.VMEM((feats, feats), F32)
        square16 = pltpu.VMEM((feats, feats), BF16)
        result = pl.pallas_call(
            functools.partial(kernel, n, nz),
            out_shape=[tokens16] * 4,
            in_specs=[hbm] * 8,
            out_specs=[vmem] * 4,
            scratch_shapes=[tokens16] * 8
            + [tokens32] * 6
            + [pltpu.VMEM((2 * rows, feats), BF16), pltpu.VMEM((heads, DH, rows), F32)]
            + [pltpu.VMEM((heads, rows, rows), F32), pltpu.VMEM((heads, rows, rows), BF16)]
            + [state] * 8
            + [pltpu.VMEM((8, DH), F32), pltpu.VMEM((nz, 8, DH), F32), pltpu.VMEM((8, DH), F32)]
            + [square32, pltpu.VMEM((n, slab, feats), F32)]
            + [square16] * 4
            + [
                pltpu.SMEM((n,), jnp.int32),
                pltpu.SMEM((n,), jnp.int32),
                pltpu.SMEM((heads,), F32),
                pltpu.VMEM((1, feats), F32),
                pltpu.SemaphoreType.DMA((8,)),
                pltpu.SemaphoreType.DMA((5,)),
                pltpu.SemaphoreType.DMA((5,)),
                pltpu.SemaphoreType.REGULAR((3,)),
            ],
            compiler_params=pltpu.CompilerParams(
                collective_id=0, has_side_effects=True, vmem_limit_bytes=24 << 20
            ),
        )(
            *[
                pltpu.with_memory_space_constraint(x, pltpu.HBM)
                for x in (
                    block_length,
                    parent,
                    decay_rate,
                    norm_gain.reshape(1, feats),
                    queries,
                    key_tokens,
                    values,
                    upstream,
                )
            ]
        )
        return pl.pallas_call(
            publish,
            out_shape=[jax.ShapeDtypeStruct((rows, feats), BF16)] * 4,
            in_specs=[vmem] * 4,
            out_specs=[hbm] * 4,
            scratch_shapes=[pltpu.SemaphoreType.DMA((4,))],
            compiler_params=pltpu.CompilerParams(has_side_effects=True, vmem_limit_bytes=1 << 20),
        )(*[pltpu.with_memory_space_constraint(x, pltpu.VMEM) for x in result])

    tokens = P("seg", "head")
    return jax.shard_map(
        local,
        mesh=mesh,
        in_specs=(tokens, tokens, tokens, tokens, P("head"), P("head"), P(), P()),
        out_specs=(tokens,) * 4,
        check_vma=False,
    )
```

```python
import functools

import jax
import jax.numpy as jnp
from jax import lax
from jax.experimental import pallas as pl
from jax.experimental.pallas import tpu as pltpu
from jax.sharding import PartitionSpec as P

F32 = jnp.float32
BF16 = jnp.bfloat16
MESH = pl.DeviceIdType.MESH
norm_eps = 1e-05
DH = 128
QUADS = ((0, 0), (1, 0), (1, 1))


def mm(a, b, ca, cb):
    return lax.dot_general(a, b, (((ca,), (cb,)), ((), ())), preferred_element_type=F32)


def split(x):
    hi = x.astype(BF16)
    return hi, (x - hi.astype(F32)).astype(BF16)


def iota(shape, dim):
    return lax.broadcasted_iota(jnp.int32, shape, dim)


def chip_peers(chip, count):
    if count != 16:
        return [lax.rem(chip + i, count) for i in range(1, count)]
    y, x = lax.div(chip, 4), lax.rem(chip, 4)
    ys = [lax.rem(y + d, 4) * 4 for d in range(4)]
    xs = [lax.rem(x + d, 4) for d in range(4)]
    hops = (0, 1, 2, 1)
    steps = [(dy, dx) for dy in range(4) for dx in range(4)]
    steps.sort(key=lambda s: -(hops[s[0]] + hops[s[1]]))
    return [ys[dy] + xs[dx] for dy, dx in steps[:-1]]


def both(a, dim):
    return jnp.concatenate([a, a], axis=dim)


def diagonal(blocks):
    none = jnp.zeros_like(blocks[0])
    return jnp.concatenate(
        [
            jnp.concatenate([b if j == i else none for j in range(len(blocks))], axis=1)
            for i, b in enumerate(blocks)
        ],
        axis=0,
    )


def head_peers(z, nz):
    steps = sorted(range(1, nz), key=lambda d: -min(d, nz - d))
    return [lax.rem(z + d, nz) for d in steps]


def kernel(
    n,
    nz,
    length_hbm,
    parent_hbm,
    rate_hbm,
    gain_hbm,
    q_hbm,
    k_hbm,
    v_hbm,
    u_hbm,
    ob,
    dqb,
    dkb,
    dvb,
    qm,
    km,
    vm,
    um,
    dab,
    kend,
    vend,
    qfade,
    sc,
    att,
    da,
    qscale,
    dkl,
    dvl,
    pair,
    qst,
    dec,
    wgt,
    state_out,
    state_in,
    carry_out,
    carry_in,
    grad_out,
    grad_in,
    back_out,
    back_in,
    zsend,
    zrecv,
    scalars_ref,
    tree,
    tree_gain,
    whi,
    wlo,
    thi,
    tlo,
    length_ref,
    parent_ref,
    rate_ref,
    gain_ref,
    in_sem,
    send_sem,
    recv_sem,
    token,
):
    me = lax.axis_index("seg")
    z = lax.axis_index("head")
    rows, feats = qm.shape
    heads = feats // DH
    half = rows // 2
    chunk = DH
    chunks = rows // chunk
    slab = state_out.shape[1]
    per_head = DH // slab
    width = float(feats * nz)

    loads = [
        pltpu.make_async_copy(src, dst, in_sem.at[i])
        for i, (src, dst) in enumerate(
            (
                (k_hbm, km),
                (length_hbm, length_ref),
                (rate_hbm, rate_ref),
                (v_hbm, vm),
                (parent_hbm, parent_ref),
                (q_hbm, qm),
                (u_hbm, um),
                (gain_hbm, gain_ref),
            )
        )
    ]
    for load in loads:
        load.start()

    barrier = pltpu.get_barrier_semaphore()
    chip, core = lax.div(me, heads), lax.rem(me, heads)
    chips = chip_peers(chip, per_head)
    peers = [c * heads + h for c in chips for h in range(heads)]
    peers += [chip * heads + lax.rem(core + h, heads) for h in range(1, heads)]
    lines = head_peers(z, nz)

    def greet(sem, peer):
        pl.semaphore_signal(sem, inc=1, device_id=peer, device_id_type=MESH)

    def along(step):
        return (me, lax.rem(z + step, nz)), (me, lax.rem(z + nz - step, nz))

    for peer in peers:
        greet(barrier, (peer, z))
    for peer in along(1):
        greet(barrier, peer)

    def push(src, dst, which, peer):
        pltpu.make_async_remote_copy(
            src_ref=src,
            dst_ref=dst,
            send_sem=send_sem.at[which],
            recv_sem=recv_sem.at[which],
            device_id=(peer, z),
            device_id_type=MESH,
        ).start()

    def scatter(src, dst, which, h):
        for c in chips:
            push(src.at[h * per_head + c], dst.at[me], which, c * heads + h)

    def scatter_near(src, dst, which):
        for step in range(1, heads):
            h = lax.rem(core + step, heads)
            push(src.at[h * per_head + chip], dst.at[me], which, chip * heads + h)
        dst[me] = src[core * per_head + chip]

    def give_back(src, dst, which):
        slot = core * per_head + chip
        for peer in peers:
            push(src.at[peer], dst.at[slot], which, peer)
        dst[slot] = src[me]

    def every(src, dst, which, count):
        return pltpu.make_async_remote_copy(
            src_ref=src.at[pl.ds(0, count)],
            dst_ref=dst.at[pl.ds(0, count)],
            send_sem=send_sem.at[which],
            recv_sem=recv_sem.at[which],
            device_id=(me, z),
            device_id_type=MESH,
        )

    for load in loads[:4]:
        load.wait()
    length = length_ref[me].astype(F32)
    rates = [rate_ref[h] for h in range(heads)]
    at_row = iota((1, rows), 1).astype(F32)
    for h in range(heads):
        lanes = slice(h * DH, (h + 1) * DH)
        end = jnp.where(at_row < length, jnp.exp(-rates[h] * (length - 1.0 - at_row)), 0.0)
        faded = (km[:, lanes].T.astype(F32) * end).astype(BF16)
        total = mm(faded, vm[:, lanes], 1, 0)
        state_out[h * per_head : (h + 1) * per_head] = total.reshape(per_head, slab, DH)

    pl.semaphore_wait(barrier, n - 1 + 2)
    for h in range(heads):
        scatter(state_out, state_in, 0, h)
    scatter_near(state_out, state_in, 0)
    for peer in along(1):
        greet(token.at[0], peer)

    for load in loads[4:]:
        load.wait()
    own_rate = rate_ref[core]
    place = jnp.where(
        iota((slab, feats), 1) % slab == iota((slab, feats), 0), iota((slab, feats), 1) // slab, -2
    )
    tree[pl.ds(0, slab), :] = jnp.zeros((slab, feats), F32)
    tree_gain[0] = jnp.zeros((slab, feats), F32)
    for b in range(1, n):
        p = parent_ref[b]
        branch = jnp.where(place == p, 1.0, 0.0) + tree_gain[jnp.maximum(p, 0)]
        tree[b * slab : (b + 1) * slab, :] = branch
        fade = jnp.exp(jnp.full((slab, feats), -own_rate * length_ref[b].astype(F32)))
        tree_gain[b] = branch * fade
    hi, lo = split(tree[...])
    whi[...] = hi
    wlo[...] = lo

    used = iota((rows, feats), 0).astype(F32) < length
    for ref in (qm, km, vm):
        ref[...] = jnp.where(used, ref[...].astype(F32), 0.0).astype(BF16)

    def attend(h):
        lanes = slice(h * DH, (h + 1) * DH)
        for i, j in QUADS:
            up, low = slice(i * half, (i + 1) * half), slice(j * half, (j + 1) * half)
            raw = mm(qm[up, lanes], km[low, lanes], 1, 1)
            space = (iota((half, half), 0) - iota((half, half), 1) + (i - j) * half).astype(F32)
            decay = jnp.where(space >= 0.0, jnp.exp(-rates[h] * jnp.maximum(space, 0.0)), 0.0)
            weighted = (raw * decay).astype(BF16)
            dec[h, up, low] = decay
            wgt[h, up, low] = weighted
            local = mm(weighted, vm[low, lanes], 1, 0)
            att[up, lanes] = local if j == 0 else att[up, lanes] + local

    def combine(src, dst, hi, lo):
        x = src[...].reshape(n * slab, DH).astype(BF16)
        result = mm(jnp.concatenate([hi[...], lo[...]], axis=1), both(x, 0), 1, 0)
        dst[...] = result.reshape(n, slab, DH)

    attend(0)
    pl.semaphore_wait(token.at[0], 2)
    for peer in along(2):
        greet(token.at[1], peer)
    every(state_out, state_in, 0, n - 1).wait_recv()
    combine(state_in, carry_out, whi, wlo)
    give_back(carry_out, carry_in, 1)

    for h in range(1, heads):
        attend(h)
    scaled = um[...].astype(F32) * gain_ref[...]
    sc[...] = scaled
    pair[0:rows, :] = scaled.astype(BF16)
    at_col = iota((rows, DH), 0).astype(F32)
    for h in range(heads):
        lanes = slice(h * DH, (h + 1) * DH)
        fade = jnp.exp(-rates[h] * (at_col + 1.0))
        qscale[:, lanes] = fade
        qfade[:, lanes] = (qm[:, lanes].astype(F32) * fade).astype(BF16)
        end = jnp.exp(-rates[h] * jnp.maximum(length - 1.0 - at_col, 0.0))
        kend[:, lanes] = (km[:, lanes].astype(F32) * end).astype(BF16)
        vend[:, lanes] = (vm[:, lanes].astype(F32) * end).astype(BF16)
        qst[h] = qm[:, lanes].T.astype(F32) * jnp.exp(-rates[h] * (at_row + 1.0))
    hi, lo = split(tree[...].T)
    thi[...] = hi
    tlo[...] = lo
    pl.semaphore_wait(token.at[1], 2)
    for peer in along(4):
        greet(token.at[2], peer)
    every(carry_out, carry_in, 1, n - 1).wait_recv()

    def carried(h):
        return carry_in[h * per_head : (h + 1) * per_head].reshape(DH, DH)

    entering = diagonal([carried(h).astype(BF16) for h in range(heads)])
    brought = mm(qfade[...], entering, 1, 0)
    row = iota((8, DH), 0)
    block = iota((8, 2 * chunks * DH), 1) // DH
    chosen = iota((8, 2 * chunks * DH), 0) == block // 2 + (block % 2) * chunks
    folded = []
    for c in range(chunks):
        part = slice(c * chunk, (c + 1) * chunk)
        a = att[part, :] + brought[part]
        att[part, :] = a
        pair[rows + c * chunk : rows + (c + 1) * chunk, :] = a.astype(BF16)
        square, inner = a * a, a * sc[part, :]
        square = sum(square[:, h * DH : (h + 1) * DH] for h in range(heads))
        inner = sum(inner[:, h * DH : (h + 1) * DH] for h in range(heads))
        folded += [square.astype(BF16), inner.astype(BF16)]
    pick = jnp.where(chosen, 1.0, 0.0).astype(BF16)
    message = mm(pick, jnp.concatenate(folded, axis=1), 1, 1)
    zsend[...] = message
    pl.semaphore_wait(token.at[2], 2)
    for peer in lines:
        pltpu.make_async_remote_copy(
            src_ref=zsend,
            dst_ref=zrecv.at[z],
            send_sem=send_sem.at[4],
            recv_sem=recv_sem.at[4],
            device_id=(me, peer),
            device_id_type=MESH,
        ).start()
    zrecv[z] = message
    every(zrecv, zrecv, 4, nz - 1).wait_recv()
    sums = jnp.sum(zrecv[...], axis=0)
    inverse = lax.rsqrt(sums / width + norm_eps)
    slope = inverse * inverse * inverse * pltpu.roll(sums, chunks, 0) / width

    for h in range(heads):
        lanes = slice(h * DH, (h + 1) * DH)
        parts = []
        for scalars in (inverse, -slope):
            for c in range(chunks):
                piece = qst[h, :, c * chunk : (c + 1) * chunk] * scalars[c : c + 1, :]
                parts.append(piece.astype(BF16))
        grad = mm(jnp.concatenate(parts, axis=1), pair[:, lanes], 1, 0)
        grad_out[h * per_head : (h + 1) * per_head] = grad.reshape(per_head, slab, DH)
        scatter(grad_out, grad_in, 2, h)
    scatter_near(grad_out, grad_in, 2)

    scalars_ref[...] = jnp.where(row < chunks, inverse, pltpu.roll(slope, chunks, 0))

    def local_gradients():
        columns = jnp.concatenate([scalars_ref[...]] * (DH // 8), axis=0).T
        for c in range(chunks):
            part = slice(c * chunk, (c + 1) * chunk)
            inv, bend = columns[:, c : c + 1], columns[:, chunks + c : chunks + c + 1]
            a = att[part, :]
            grad = inv * sc[part, :] - bend * a
            da[part, :] = grad
            dab[part, :] = grad.astype(BF16)
            ob[part, :] = (a * inv * gain_ref[...]).astype(BF16)

    def pull(h):
        lanes = slice(h * DH, (h + 1) * DH)
        dq = [None, None]
        dk = [None, None]
        dv = [None, None]

        def added(sums, at, term):
            sums[at] = term if sums[at] is None else sums[at] + term

        for i, j in QUADS:
            up, low = slice(i * half, (i + 1) * half), slice(j * half, (j + 1) * half)
            grad = dab[up, lanes]
            dweighted = mm(grad, vm[low, lanes], 1, 1).astype(BF16).astype(F32)
            draw = (dweighted * dec[h, up, low]).astype(BF16)
            added(dq, i, mm(draw, km[low, lanes], 1, 0))
            added(dk, j, mm(draw, qm[up, lanes], 0, 0))
            added(dv, j, mm(wgt[h, up, low], grad, 0, 0))
        chi, clo = split(carried(h))
        for i in range(2):
            part = slice(i * half, (i + 1) * half)
            ghi, glo = split(da[part, lanes])
            through = mm(both(ghi, 1), jnp.concatenate([chi, clo], axis=1), 1, 1) + mm(glo, chi, 1, 1)
            total = dq[i] + through * qscale[part, lanes]
            inside = iota((half, DH), 0).astype(F32) < length - float(i * half)
            dqb[part, lanes] = jnp.where(inside, total, 0.0).astype(BF16)
            dkl[part, lanes] = dk[i]
            dvl[part, lanes] = dv[i]

    @pl.when(me >= 0)
    def _():
        local_gradients()
        pull(0)

    every(grad_out, grad_in, 2, n - 1).wait_recv()
    combine(grad_in, back_out, thi, tlo)
    give_back(back_out, back_in, 3)
    for h in range(1, heads):
        pull(h)
    every(back_out, back_in, 3, n - 1).wait_recv()

    leaving = diagonal(
        [
            back_in[h * per_head : (h + 1) * per_head].reshape(DH, DH).astype(BF16)
            for h in range(heads)
        ]
    )
    dkb[...] = (dkl[...] + mm(vend[...], leaving, 1, 1)).astype(BF16)
    dvb[...] = (dvl[...] + mm(kend[...], leaving, 1, 0)).astype(BF16)
    for which, src in enumerate((state_out, carry_out, grad_out, back_out)):
        every(src, src, which, n - 1).wait_send()
    every(zrecv, zrecv, 4, nz - 1).wait_send()


def publish(*refs):
    count = (len(refs) - 1) // 2
    copies = [
        pltpu.make_async_copy(refs[i], refs[count + i], refs[-1].at[i]) for i in range(count)
    ]
    for copy in copies:
        copy.start()
    for copy in copies:
        copy.wait()


def solution(mesh):
    n, nz = mesh.shape["seg"], mesh.shape["head"]

    def local(queries, key_tokens, values, upstream, norm_gain, decay_rate, block_length, parent):
        rows, feats = queries.shape
        heads = feats // DH
        slab = feats // n
        hbm = pl.BlockSpec(memory_space=pltpu.HBM)
        vmem = pl.BlockSpec(memory_space=pltpu.VMEM)
        tokens16 = pltpu.VMEM((rows, feats), BF16)
        tokens32 = pltpu.VMEM((rows, feats), F32)
        state = pltpu.VMEM((n, slab, DH), F32)
        square32 = pltpu.VMEM((feats, feats), F32)
        square16 = pltpu.VMEM((feats, feats), BF16)
        result = pl.pallas_call(
            functools.partial(kernel, n, nz),
            out_shape=[tokens16] * 4,
            in_specs=[hbm] * 8,
            out_specs=[vmem] * 4,
            scratch_shapes=[tokens16] * 8
            + [tokens32] * 6
            + [pltpu.VMEM((2 * rows, feats), BF16), pltpu.VMEM((heads, DH, rows), F32)]
            + [pltpu.VMEM((heads, rows, rows), F32), pltpu.VMEM((heads, rows, rows), BF16)]
            + [state] * 8
            + [pltpu.VMEM((8, DH), F32), pltpu.VMEM((nz, 8, DH), F32), pltpu.VMEM((8, DH), F32)]
            + [square32, pltpu.VMEM((n, slab, feats), F32)]
            + [square16] * 4
            + [
                pltpu.SMEM((n,), jnp.int32),
                pltpu.SMEM((n,), jnp.int32),
                pltpu.SMEM((heads,), F32),
                pltpu.VMEM((1, feats), F32),
                pltpu.SemaphoreType.DMA((8,)),
                pltpu.SemaphoreType.DMA((5,)),
                pltpu.SemaphoreType.DMA((5,)),
                pltpu.SemaphoreType.REGULAR((3,)),
            ],
            compiler_params=pltpu.CompilerParams(
                collective_id=0, has_side_effects=True, vmem_limit_bytes=24 << 20
            ),
        )(
            *[
                pltpu.with_memory_space_constraint(x, pltpu.HBM)
                for x in (
                    block_length,
                    parent,
                    decay_rate,
                    norm_gain.reshape(1, feats),
                    queries,
                    key_tokens,
                    values,
                    upstream,
                )
            ]
        )
        return pl.pallas_call(
            publish,
            out_shape=[jax.ShapeDtypeStruct((rows, feats), BF16)] * 4,
            in_specs=[vmem] * 4,
            out_specs=[hbm] * 4,
            scratch_shapes=[pltpu.SemaphoreType.DMA((4,))],
            compiler_params=pltpu.CompilerParams(has_side_effects=True, vmem_limit_bytes=1 << 20),
        )(*[pltpu.with_memory_space_constraint(x, pltpu.VMEM) for x in result])

    tokens = P("seg", "head")
    return jax.shard_map(
        local,
        mesh=mesh,
        in_specs=(tokens, tokens, tokens, tokens, P("head"), P("head"), P(), P()),
        out_specs=(tokens,) * 4,
        check_vma=False,
    )
```
